256 devices in a mesh: region: 16 (over y, x_hi, core), member: 16 (over x_lo, z).
Axes of the slice: x: 4 (x_hi: 2, x_lo: 2; x = x_hi * 2 + x_lo), y: 4, z: 8, core: 2. Of those that a mesh axis runs over, the one named last changes fastest.
Arguments:
- prior_states: float32 [32, 256, 16, 2048], P('region', 'member'), may hold values from -6 to 6
- prior_in_sensor_space: float32 [32, 256, 256], P('region', 'member'), may hold values from -10 to 10
- sensor_readings: float32 [32, 256], replicated, may hold values from -8 to 8
- error_precisions: float32 [32, 256], replicated, may hold values from 0.25 to 4
- live_tallies: int32 [32], replicated, may hold values from 1 to 256
- adjacent_areas: int32 [32, 4], replicated, may hold values from 0 to 31, as said below
- taper_lookup: int32 [32, 5, 256], replicated, may hold values from 0 to 15
- blend_lookup: int32 [32, 16, 5], P('region', 'member'), may hold values from 0 to 15
- taper_factors: float32 [16], replicated, may hold values from 0.05 to 1
Outputs:
- analysis: float32 [32, 256, 16, 2048], P('region', 'member')
The draws below stay inside these ranges and needn't reach their ends.
Inputs may be any that keep to these rules, and one draw needn't show every extreme that they name: `adjacent_areas`: the 4 neighbours of region r are distinct, differ from r, and each neighbour q satisfies (q // 2 - r // 2) equal to -1, 0 or 1 modulo 32 // 2.
All inputs are finite; a program needn't handle non-finite values.
Results may differ from the reference program's by a relative error of at most 0.0003.
Values sent between devices are 32-bit elements; how exact they have to be, the bound alone decides.
No kernel may reach another device: no remote copies, remote signals or barrier semaphores. Data moves between devices by JAX's collectives and lax.ppermute only.
A program may use at most 64 MiB of HBM per device.

```python
import math
import jax
import jax.numpy as jnp
from jax import lax

MEMBER_TOTAL = 256
NOBS = 256
NBR = 4
LEVELS = 16
NSIT = 8
REG_DEV = 2
TILE_POINTS = 2048
AREA_TOTAL = 32
TILES_PER_AREA = 16


def draw_adjacent_areas(key, part):
    slot_count = 3 * REG_DEV
    dev_count = AREA_TOTAL // REG_DEV
    area_batch = jnp.arange(AREA_TOTAL, dtype=jnp.int32)
    own_slot = REG_DEV + area_batch % REG_DEV
    slot_ids = jnp.arange(slot_count, dtype=jnp.int32)
    scores = jax.random.randint(jax.random.fold_in(key, 11), (AREA_TOTAL, slot_count), 0, 1 << 20, dtype=jnp.int32) * slot_count + slot_ids[None, :]
    scores = jnp.where(slot_ids[None, :] == own_slot[:, None], 1 << 30, scores)
    chosen = jnp.argsort(scores, axis=1, stable=True)[:, :NBR].astype(jnp.int32)
    device = area_batch // REG_DEV
    target = (device[:, None] + chosen // REG_DEV - 1) % dev_count * REG_DEV + chosen % REG_DEV
    return target.astype(jnp.int32)


def draw_prior_in_sensor_space(key, part):
    noise_key = jax.random.fold_in(key, 21)
    member_key = jax.random.fold_in(key, 22)
    column_key = jax.random.fold_in(key, 23)
    column_mode = jnp.clip(jax.random.normal(column_key, (AREA_TOTAL, NOBS), jnp.float32), -3.0, 3.0)
    noise = jnp.clip(jax.random.normal(noise_key, (AREA_TOTAL, MEMBER_TOTAL, NOBS), jnp.float32), -4.0, 4.0)
    member_mode = jnp.clip(jax.random.normal(member_key, (MEMBER_TOTAL,), jnp.float32), -3.0, 3.0)
    strength = 0.8
    values = noise + strength * member_mode[None, :, None] * column_mode[:, None, :]
    return jnp.clip(values, -10.0, 10.0).astype(jnp.float32)


def plant(result, own_key, low, top_value):
    spot = [jax.random.randint(jax.random.fold_in(own_key, axis), (), 0, length) for axis, length in enumerate(result.shape)]
    widest = result.shape.index(max(result.shape))
    neighbour = spot[:widest] + [(spot[widest] + 1) % result.shape[widest]] + spot[widest + 1:]
    return result.at[tuple(spot)].set(low).at[tuple(neighbour)].set(top_value)


def block_scale(stream_key, dims, pieces, least, largest):
    def one(dim, parts):
        heights = jax.random.uniform(jax.random.fold_in(jax.random.fold_in(stream_key, 6), dim), (parts,), jnp.float32, least / len(pieces), largest / len(pieces))
        return jnp.repeat(jnp.exp(heights), dims[dim] // parts).reshape((-1,) + (1,) * (len(dims) - dim - 1))

    gain = one(*pieces[0])
    for cut in pieces[1:]:
        gain = gain * one(*cut)
    return gain


def bell_draw(rng, shape, deviation, most, cuts=(), kind=jnp.bfloat16):
    drawn = jax.random.normal(rng, shape, jnp.float32) * deviation
    if len(cuts) > 0:
        drawn = block_scale(rng, shape, cuts, -0.22, 0.18) * drawn
    return jnp.clip(drawn, min=-most, max=most).astype(kind)


def setup_inputs(seed: int = 0) -> dict:
    key_of = jax.random.split(jax.random.key(seed), 10)
    return {
        "prior_states": bell_draw(key_of[0], (AREA_TOTAL, MEMBER_TOTAL, TILES_PER_AREA, TILE_POINTS), 1.0, 6.0, ((0, 16), (1, 16)), jnp.float32),
        "prior_in_sensor_space": draw_prior_in_sensor_space(jax.random.fold_in(key_of[9], 71), 0),
        "sensor_readings": bell_draw(key_of[2], (AREA_TOTAL, NOBS), 1.5, 8.0, (), jnp.float32),
        "error_precisions": jnp.clip(jnp.exp(jax.random.uniform(key_of[3], (AREA_TOTAL, NOBS), jnp.float32, math.log(0.25), math.log(4.0))), 0.25, 4.0),
        "live_tallies": plant(jax.random.randint(key_of[4], (AREA_TOTAL,), 1, NOBS + 1), jax.random.fold_in(key_of[4], 1), 1, NOBS).astype(jnp.int32),
        "adjacent_areas": draw_adjacent_areas(jax.random.fold_in(key_of[9], 71), 0),
        "taper_lookup": plant(jax.random.randint(key_of[6], (AREA_TOTAL, NBR + 1, NOBS), 0, LEVELS), jax.random.fold_in(key_of[6], 1), 0, LEVELS - 1).astype(jnp.int32),
        "blend_lookup": plant(jax.random.randint(key_of[7], (AREA_TOTAL, TILES_PER_AREA, NBR + 1), 0, LEVELS), jax.random.fold_in(key_of[7], 1), 0, LEVELS - 1).astype(jnp.int32),
        "taper_factors": jnp.clip(jnp.exp(jax.random.uniform(key_of[8], (LEVELS,), jnp.float32, math.log(0.05), math.log(1.0))), 0.05, 1.0),
    }


inflation = 1.1
highest = lax.Precision.HIGHEST

def newton_root(gram_mat):
    order = gram_mat.shape[-1]
    identity = jnp.eye(order, dtype=jnp.float32)
    norm_value = jnp.sqrt(lax.optimization_barrier(jnp.sum(gram_mat * gram_mat, axis=(-2, -1))))
    scaled = gram_mat / norm_value[..., None, None]
    root_mat = jnp.broadcast_to(identity, gram_mat.shape)
    for sweep in range(NSIT):
        correction = 1.5 * identity - 0.5 * jnp.einsum('...ij,...jk->...ik', root_mat, scaled, precision=highest)
        root_mat = jnp.einsum('...ij,...jk->...ik', correction, root_mat, precision=highest)
        if sweep + 1 < NSIT:
            scaled = jnp.einsum('...ij,...jk->...ik', scaled, correction, precision=highest)
    return (root_mat, norm_value)

def transform_of(gram_mat, drive_vec):
    members = gram_mat.shape[-1]
    root_mat, norm_value = newton_root(gram_mat)
    half_way = jnp.einsum('...jk,...k->...j', root_mat, drive_vec, precision=highest)
    mean_shift = jnp.einsum('...jk,...k->...j', root_mat, half_way, precision=highest) / norm_value[..., None]
    factor = jnp.sqrt(members - 1.0) / jnp.sqrt(norm_value)
    return factor[..., None, None] * root_mat + mean_shift[..., None]

def reference(prior_states, prior_in_sensor_space, sensor_readings, error_precisions, live_tallies, adjacent_areas, taper_lookup, blend_lookup, taper_factors):
    ens_mean = lax.optimization_barrier(jnp.mean(prior_in_sensor_space, axis=1))
    perturb = prior_in_sensor_space - ens_mean[:, None, :]
    live_mask = (jnp.arange(NOBS, dtype=jnp.int32)[None, :] < live_tallies[:, None]).astype(jnp.float32)
    obs_weight = error_precisions * live_mask
    innovation = sensor_readings - ens_mean
    blocks = jnp.concatenate([jnp.arange(AREA_TOTAL, dtype=jnp.int32)[:, None], adjacent_areas.astype(jnp.int32)], axis=1).astype(jnp.int32)
    local_weight = jnp.take(taper_factors, taper_lookup, axis=0)
    identity = jnp.eye(MEMBER_TOTAL, dtype=jnp.float32)

    def one_region(area_batch):
        chosen = blocks[area_batch]
        pert_sel = jnp.take(perturb, chosen, axis=0)
        weight_sel = jnp.take(obs_weight, chosen, axis=0) * local_weight[area_batch]
        innov_sel = jnp.take(innovation, chosen, axis=0)
        weighted = pert_sel * weight_sel[:, None, :]
        gram_mat = jnp.einsum('bkm,bjm->kj', weighted, pert_sel, precision=highest) + (MEMBER_TOTAL - 1) / inflation * identity
        drive_vec = jnp.einsum('bkm,bm->k', weighted, innov_sel, precision=highest)
        return transform_of(gram_mat, drive_vec)
    transforms = lax.map(one_region, jnp.arange(AREA_TOTAL, dtype=jnp.int32))
    blend_weight = jnp.take(taper_factors, blend_lookup, axis=0)
    blend_weight = blend_weight / lax.optimization_barrier(jnp.sum(blend_weight, axis=-1, keepdims=True))

    def update_region(area_batch):
        picked = jnp.take(transforms, blocks[area_batch], axis=0)
        patch_transform = jnp.einsum('qb,bjk->qjk', blend_weight[area_batch], picked, precision=highest)
        area_sorted = prior_states[area_batch]
        center = lax.optimization_barrier(jnp.mean(area_sorted, axis=0, keepdims=True))
        return center + jnp.einsum('qjk,jqv->kqv', patch_transform, area_sorted - center, precision=highest)
    return lax.map(update_region, jnp.arange(AREA_TOTAL, dtype=jnp.int32))
```

```python
import jax
import jax.numpy as jnp
from jax import lax
from jax.sharding import PartitionSpec as P

MEMBER_TOTAL = 256
NOBS = 256
NSIT = 8
REG_DEV = 2
LEVELS = 16

inflation = 1.1
highest = lax.Precision.HIGHEST


def table_lookup(table, index):
    out = jnp.zeros(index.shape, table.dtype)
    for level in range(LEVELS):
        out = jnp.where(index == level, table[level], out)
    return out


def gather_members(array, dim):
    peers = lax.axis_size("member")
    pieces = lax.all_to_all(
        jnp.broadcast_to(array[None], (peers, *array.shape)), "member", 0, 0, tiled=True
    )
    shape = list(array.shape)
    shape[dim] *= peers
    return jnp.moveaxis(pieces, 0, dim).reshape(shape)


def extended(cells):
    count = lax.axis_size("region")
    return jnp.concatenate(
        [
            lax.ppermute(cells, "region", [(i, (i + 1) % count) for i in range(count)]),
            cells,
            lax.ppermute(cells, "region", [((i + 1) % count, i) for i in range(count)]),
        ],
        axis=0,
    )


def newton_root(gram_mat):
    order = gram_mat.shape[-1]
    identity = jnp.eye(order, dtype=jnp.float32)
    norm_value = jnp.sqrt(jnp.sum(gram_mat * gram_mat, axis=(-2, -1)))
    scaled = gram_mat / norm_value[..., None, None]
    root_mat = jnp.broadcast_to(identity, gram_mat.shape)
    for sweep in range(NSIT):
        correction = 1.5 * identity - 0.5 * jnp.einsum(
            "...ij,...jk->...ik", root_mat, scaled, precision=highest
        )
        root_mat = jnp.einsum("...ij,...jk->...ik", correction, root_mat, precision=highest)
        if sweep + 1 < NSIT:
            scaled = jnp.einsum("...ij,...jk->...ik", scaled, correction, precision=highest)
    return (root_mat, norm_value)


def transform_of(gram_mat, drive_vec):
    members = gram_mat.shape[-1]
    root_mat, norm_value = newton_root(gram_mat)
    half_way = jnp.einsum("...jk,...k->...j", root_mat, drive_vec, precision=highest)
    mean_shift = (
        jnp.einsum("...jk,...k->...j", root_mat, half_way, precision=highest)
        / norm_value[..., None]
    )
    factor = jnp.sqrt(members - 1.0) / jnp.sqrt(norm_value)
    return factor[..., None, None] * root_mat + mean_shift[..., None]


def body(
    prior_states,
    prior_in_sensor_space,
    sensor_readings,
    error_precisions,
    live_tallies,
    adjacent_areas,
    taper_lookup,
    blend_lookup,
    taper_factors,
):
    whole = gather_members(prior_in_sensor_space, 1)
    states = []
    for region in range(REG_DEV):
        by_patch = jnp.swapaxes(prior_states[region], 0, 1)
        moved = lax.all_to_all(by_patch, "member", 0, 0, tiled=True)
        states.append(moved.reshape(MEMBER_TOTAL, -1))

    region_pos = lax.axis_index("region")
    cycle_size = lax.axis_size("region")
    local_nbr = lax.dynamic_slice_in_dim(adjacent_areas, region_pos * REG_DEV, REG_DEV, 0)
    nbr_slot = (local_nbr // REG_DEV - region_pos + 1) % cycle_size * REG_DEV + local_nbr % REG_DEV
    own_slot = REG_DEV + jnp.arange(REG_DEV, dtype=jnp.int32)
    slot_table = jnp.concatenate([own_slot[:, None], nbr_slot], axis=1)
    slot_ids = jnp.arange(3 * REG_DEV, dtype=jnp.int32)
    candidate = (region_pos - 1 + slot_ids // REG_DEV) % cycle_size * REG_DEV + slot_ids % REG_DEV
    columns = extended(whole)
    live_mask = (jnp.arange(NOBS, dtype=jnp.int32)[None, :] < live_tallies[:, None]).astype(
        jnp.float32
    )
    obs_weight = error_precisions * live_mask
    weight_cand = jnp.take(obs_weight, candidate, axis=0)
    value_cand = jnp.take(sensor_readings, candidate, axis=0)
    local_loc = lax.dynamic_slice_in_dim(taper_lookup, region_pos * REG_DEV, REG_DEV, 0)
    loc_weight = table_lookup(taper_factors, local_loc)
    ens_mean = jnp.mean(columns, axis=1)
    perturb = columns - ens_mean[:, None, :]
    innovation = value_cand - ens_mean
    pert_sel = jnp.take(perturb, slot_table, axis=0)
    weight_sel = jnp.take(weight_cand, slot_table, axis=0) * loc_weight
    innov_sel = jnp.take(innovation, slot_table, axis=0)
    weighted = pert_sel * weight_sel[:, :, None, :]
    gram_part = jnp.einsum("rbkm,rbjm->rkj", weighted, pert_sel, precision=highest)
    drive_part = jnp.einsum("rbkm,rbm->rk", weighted, innov_sel, precision=highest)
    identity = jnp.eye(MEMBER_TOTAL, dtype=jnp.float32)
    gram_mat = gram_part + (MEMBER_TOTAL - 1) / inflation * identity
    transforms = transform_of(gram_mat, drive_part)
    nearby = extended(transforms)
    blend_weight = table_lookup(taper_factors, blend_lookup[:, 0])
    blend_weight = blend_weight / jnp.sum(blend_weight, axis=-1, keepdims=True)

    finished = []
    for region in range(REG_DEV):
        picked = jnp.take(nearby, slot_table[region], axis=0)
        patch_transform = jnp.sum(blend_weight[region][:, None, None] * picked, axis=0)
        center = jnp.mean(states[region], axis=0, keepdims=True)
        updated = center + jnp.einsum(
            "jk,jv->kv", patch_transform, states[region] - center, precision=highest
        )
        pieces = updated.reshape(lax.axis_size("member"), -1, updated.shape[-1])
        back = lax.all_to_all(pieces, "member", 0, 0, tiled=True)
        finished.append(jnp.swapaxes(back, 0, 1))
    return jnp.stack(finished)


def solution(mesh):
    placed = (
        P("region", "member", None, None),
        P("region", "member", None),
        P(),
        P(),
        P(),
        P(),
        P(),
        P("region", "member", None),
        P(),
    )
    return jax.shard_map(
        body,
        mesh=mesh,
        in_specs=placed,
        out_specs=P("region", "member", None, None),
        check_vma=False,
    )
```

```python
import functools

import jax
import jax.numpy as jnp
from jax import lax
from jax.experimental import pallas as pl
from jax.experimental.pallas import tpu as pltpu
from jax.sharding import PartitionSpec as P

MEMBER_TOTAL = 256
NOBS = 256
NBR = 4
NSIT = 8
REG_DEV = 2
LEVELS = 16
TILE_POINTS = 2048
SHARES = 16
SHARE = 16
RINGS = 8

inflation = 1.1
highest = lax.Precision.HIGHEST
SMEM = pl.BlockSpec(memory_space=pltpu.SMEM)


def dot(a, b):
    return lax.dot_general(
        a, b, (((1,), (0,)), ((), ())), precision=highest, preferred_element_type=jnp.float32
    )


def dot_rows(a, b):
    return lax.dot_general(
        a, b, (((1,), (1,)), ((), ())), precision=highest, preferred_element_type=jnp.float32
    )


def column_block(ref):
    width = ref.shape[-1]
    return pl.ds(pl.multiple_of(pl.program_id(0) * width, width), width)


def pack_kernel(x_ref, o_ref):
    o_ref[...] = jnp.swapaxes(x_ref[0], 0, 1)


def pack(states, region):
    width = 512
    return pl.pallas_call(
        pack_kernel,
        grid=(TILE_POINTS // width,),
        in_specs=[pl.BlockSpec((1, SHARE, SHARES, width), lambda i: (region, 0, 0, i))],
        out_specs=pl.BlockSpec((SHARES, SHARE, width), lambda i: (0, 0, i)),
        out_shape=pltpu.HBM((SHARES, SHARE, TILE_POINTS), jnp.float32),
        cost_estimate=pl.CostEstimate(flops=0, bytes_accessed=4 << 20, transcendentals=0),
        name="pack",
    )(states)


def unpack_kernel(x_ref, *refs):
    refs[-1][0] = jnp.swapaxes(x_ref[:, :, column_block(refs[-1])], 0, 1)


def unpack(pieces, region, target=None):
    width = 512
    extra = [] if target is None else [target]
    return pl.pallas_call(
        unpack_kernel,
        grid=(TILE_POINTS // width,),
        in_specs=[pl.BlockSpec(memory_space=pltpu.VMEM)]
        + [pl.BlockSpec(memory_space=pl.ANY)] * len(extra),
        out_specs=pl.BlockSpec((1, SHARE, SHARES, width), lambda i: (region, 0, 0, i)),
        out_shape=jax.ShapeDtypeStruct((REG_DEV, SHARE, SHARES, TILE_POINTS), jnp.float32),
        input_output_aliases={1: 0} if extra else {},
        cost_estimate=pl.CostEstimate(flops=0, bytes_accessed=4 << 20, transcendentals=0),
        name="unpack",
    )(pltpu.with_memory_space_constraint(pieces, pltpu.VMEM), *extra)


def slot_of(area, place, cycle):
    ring = lax.rem(area // REG_DEV - place + 1 + cycle, cycle)
    return ring * REG_DEV + lax.rem(area, REG_DEV)


def area_of(block, row, neighbours):
    return row if block == 0 else neighbours[row, block - 1]


def analysis_kernel(
    cycle,
    place_ref,
    live_ref,
    nbr_ref,
    factor_ref,
    prev_ref,
    own_ref,
    next_ref,
    values_ref,
    precision_ref,
    lookup_ref,
    out_ref,
    pert,
    mean,
    scaled,
    root,
):
    place = place_ref[0]
    for ring, source in enumerate((prev_ref, own_ref, next_ref)):
        for part in range(REG_DEV):
            block = source[:, part].reshape(MEMBER_TOTAL, NOBS)
            average = jnp.sum(block, axis=0, keepdims=True) * (1.0 / MEMBER_TOTAL)
            pert[ring * REG_DEV + part] = block - average
            mean[ring * REG_DEV + part] = jnp.broadcast_to(average, (8, NOBS))
    slots = lax.broadcasted_iota(jnp.int32, (1, NOBS), 1)
    rows = lax.broadcasted_iota(jnp.int32, (MEMBER_TOTAL, MEMBER_TOTAL), 0)
    cols = lax.broadcasted_iota(jnp.int32, (MEMBER_TOTAL, MEMBER_TOTAL), 1)
    identity = jnp.where(rows == cols, 1.0, 0.0).astype(jnp.float32)
    drives, norms = [], []
    for region in range(REG_DEV):
        row = place * REG_DEV + region
        lookup = lookup_ref[region]
        taper = jnp.zeros(lookup.shape, jnp.float32)
        for level in range(LEVELS):
            taper = jnp.where(lookup == level, factor_ref[level], taper)
        gram = ((MEMBER_TOTAL - 1) / inflation) * identity
        drive = jnp.zeros((MEMBER_TOTAL, 128), jnp.float32)
        for block in range(NBR + 1):
            area = area_of(block, row, nbr_ref)
            slot = slot_of(area, place, cycle)
            weight = jnp.where(slots < live_ref[area], precision_ref[pl.ds(area, 1), :], 0.0)
            weight = weight * taper[block : block + 1, :]
            offset = values_ref[pl.ds(area, 1), :] - mean[slot][0:1, :]
            block_pert = pert[slot]
            gram = gram + dot_rows(block_pert * weight, block_pert)
            drive = drive + dot_rows(
                block_pert, jnp.broadcast_to(weight * offset, (128, NOBS))
            )
        norm = jnp.sqrt(jnp.sum(gram * gram, keepdims=True))
        scaled[region] = gram / norm
        root[region] = identity
        drives.append(drive)
        norms.append(norm)

    def sweep(_, carry):
        for region in range(REG_DEV):
            step = 1.5 * identity - 0.5 * dot(root[region], scaled[region])
            root[region] = dot(step, root[region])
            scaled[region] = dot(scaled[region], step)
        return carry

    lax.fori_loop(0, NSIT, sweep, 0)
    for region in range(REG_DEV):
        root_mat = root[region]
        shift = dot(root_mat, dot(root_mat, drives[region])) / norms[region]
        factor = jnp.sqrt(jnp.float32(MEMBER_TOTAL - 1)) / jnp.sqrt(norms[region])
        out_ref[region] = factor * root_mat + jnp.concatenate([shift, shift], axis=1)


def analysis(cycle, place, live, nbr, factors, prev, own, after, values, precisions, lookup):
    whole = lambda *shape: pl.BlockSpec(shape, lambda i, *_: (0,) * len(shape))
    cells = whole(SHARES, REG_DEV, SHARE, NOBS)
    areas = values.shape[0]
    return pl.pallas_call(
        functools.partial(analysis_kernel, cycle),
        grid_spec=pltpu.PrefetchScalarGridSpec(
            num_scalar_prefetch=4,
            grid=(1,),
            in_specs=[
                cells,
                cells,
                cells,
                whole(areas, NOBS),
                whole(areas, NOBS),
                pl.BlockSpec((REG_DEV, NBR + 1, NOBS), lambda i, p, *_: (p[0], 0, 0)),
            ],
            out_specs=whole(REG_DEV, MEMBER_TOTAL, MEMBER_TOTAL),
            scratch_shapes=[
                pltpu.VMEM((3 * REG_DEV, MEMBER_TOTAL, NOBS), jnp.float32),
                pltpu.VMEM((3 * REG_DEV, 8, NOBS), jnp.float32),
                pltpu.VMEM((REG_DEV, MEMBER_TOTAL, MEMBER_TOTAL), jnp.float32),
                pltpu.VMEM((REG_DEV, MEMBER_TOTAL, MEMBER_TOTAL), jnp.float32),
            ],
        ),
        out_shape=jax.ShapeDtypeStruct((REG_DEV, MEMBER_TOTAL, MEMBER_TOTAL), jnp.float32),
        compiler_params=pltpu.CompilerParams(vmem_limit_bytes=24 << 20),
        cost_estimate=pl.CostEstimate(
            flops=70 * 6 * 2 * 256**3, bytes_accessed=3 << 20, transcendentals=0
        ),
        name="analysis",
    )(place, live, nbr, factors, prev, own, after, values, precisions, lookup)


def apply_kernel(
    cycle, region, place_ref, nbr_ref, factor_ref, blend_ref, prev_ref, own_ref, next_ref, x_ref, o_ref, mix
):
    @pl.when(pl.program_id(0) == 0)
    def _():
        place = place_ref[0]
        row = place * REG_DEV + region
        shares = [jnp.float32(0.0)] * (3 * REG_DEV)
        total = jnp.float32(0.0)
        for block in range(NBR + 1):
            slot = slot_of(area_of(block, row, nbr_ref), place, cycle)
            value = factor_ref[blend_ref[region, 0, block]]
            total = total + value
            shares = [s + jnp.where(slot == k, value, 0.0) for k, s in enumerate(shares)]
        acc = jnp.zeros((MEMBER_TOTAL, MEMBER_TOTAL), jnp.float32)
        for ring, source in enumerate((prev_ref, own_ref, next_ref)):
            for part in range(REG_DEV):
                acc = acc + shares[ring * REG_DEV + part] * source[part]
        mix[...] = (acc / total).T

    states = x_ref[:, :, column_block(o_ref)].reshape(MEMBER_TOTAL, o_ref.shape[-1])
    center = jnp.sum(states, axis=0, keepdims=True) * (1.0 / MEMBER_TOTAL)
    updated = center + dot(mix[...], states - center)
    o_ref[...] = updated.reshape(o_ref.shape)


def apply(cycle, region, place, nbr, factors, blend, prev, own, after, states):
    width = 512
    matrix = pl.BlockSpec(
        (REG_DEV, MEMBER_TOTAL, MEMBER_TOTAL), lambda i: (0, 0, 0), pipeline_mode=pl.Buffered(1)
    )
    tile = pl.BlockSpec((SHARES, SHARE, width), lambda i: (0, 0, i))
    return pl.pallas_call(
        functools.partial(apply_kernel, cycle, region),
        grid=(TILE_POINTS // width,),
        in_specs=[SMEM, SMEM, SMEM, SMEM, matrix, matrix, matrix, pl.BlockSpec(memory_space=pltpu.VMEM)],
        out_specs=tile,
        out_shape=pltpu.HBM((SHARES, SHARE, TILE_POINTS), jnp.float32),
        scratch_shapes=[pltpu.VMEM((MEMBER_TOTAL, MEMBER_TOTAL), jnp.float32)],
        compiler_params=pltpu.CompilerParams(vmem_limit_bytes=24 << 20),
        cost_estimate=pl.CostEstimate(
            flops=6 * 2 * 256 * 256 * TILE_POINTS, bytes_accessed=5 << 20, transcendentals=0
        ),
        name="apply",
    )(
        place,
        nbr,
        factors,
        blend,
        prev,
        own,
        after,
        pltpu.with_memory_space_constraint(states, pltpu.VMEM),
    )


def swap_pairs(bit):
    return [(i, i ^ bit) for i in range(SHARES)]


def gather_members(cells):
    index = lax.axis_index("member")
    block = cells[None]
    for bit in (1, 2, 4, 8):
        other = lax.ppermute(block, "member", swap_pairs(bit))
        upper = (index & bit) != 0
        block = jnp.concatenate(
            [jnp.where(upper, other, block), jnp.where(upper, block, other)], axis=0
        )
    return block


def from_beside(cells):
    count = lax.axis_size("region")
    before = lax.ppermute(cells, "region", [(i, (i + 1) % count) for i in range(count)])
    after = lax.ppermute(cells, "region", [((i + 1) % count, i) for i in range(count)])
    return before, after


def body(
    prior_states,
    prior_in_sensor_space,
    sensor_readings,
    error_precisions,
    live_tallies,
    adjacent_areas,
    taper_lookup,
    blend_lookup,
    taper_factors,
):
    cycle = lax.axis_size("region")
    place = lax.axis_index("region").astype(jnp.int32)[None]
    packed = [pack(prior_states, region) for region in range(REG_DEV)]
    own = gather_members(prior_in_sensor_space)
    packed[1], own = lax.optimization_barrier((packed[1], own))
    states = [lax.all_to_all(pieces, "member", 0, 0, tiled=True) for pieces in packed]
    before, after = from_beside(own)
    transforms = analysis(
        cycle,
        place,
        live_tallies,
        adjacent_areas,
        taper_factors,
        before,
        own,
        after,
        sensor_readings,
        error_precisions,
        taper_lookup,
    )
    left, right = from_beside(transforms)
    out = None
    for region in range(REG_DEV):
        updated = apply(
            cycle,
            region,
            place,
            adjacent_areas,
            taper_factors,
            blend_lookup,
            left,
            transforms,
            right,
            states[region],
        )
        back = lax.all_to_all(updated, "member", 0, 0, tiled=True)
        out = unpack(back, region, out)
    return out


def solution(mesh):
    placed = (
        P("region", "member", None, None),
        P("region", "member", None),
        P(),
        P(),
        P(),
        P(),
        P(),
        P("region", "member", None),
        P(),
    )
    return jax.shard_map(
        body,
        mesh=mesh,
        in_specs=placed,
        out_specs=P("region", "member", None, None),
        check_vma=False,
    )
```

```python
import functools

import jax
import jax.numpy as jnp
from jax import lax
from jax.experimental import pallas as pl
from jax.experimental.pallas import tpu as pltpu
from jax.sharding import PartitionSpec as P

MEMBER_TOTAL = 256
NOBS = 256
NBR = 4
NSIT = 8
REG_DEV = 2
LEVELS = 16
TILE_POINTS = 2048
SHARES = 16
SHARE = 16
RINGS = 8

inflation = 1.1
highest = lax.Precision.HIGHEST
SMEM = pl.BlockSpec(memory_space=pltpu.SMEM)


def dot(a, b):
    return lax.dot_general(
        a, b, (((1,), (0,)), ((), ())), precision=highest, preferred_element_type=jnp.float32
    )


def dot_rows(a, b):
    return lax.dot_general(
        a, b, (((1,), (1,)), ((), ())), precision=highest, preferred_element_type=jnp.float32
    )


WIDTH = 512
HALF = SHARE // 2

LISTED = [0, 7, 1, 6, 2, 5, 3, 4, 12, 11, 13, 10, 14, 9, 15, 8]
PLACE = [LISTED.index(member) for member in range(SHARES)]


def columns(number):
    return pl.ds(number * WIDTH, WIDTH)


def pack_kernel(x_ref, o_ref):
    for number in range(TILE_POINTS // WIDTH):
        by_patch = jnp.swapaxes(x_ref[0, :, :, columns(number)], 0, 1)
        for place, patch in enumerate(LISTED):
            o_ref[place, 0, :, columns(number)] = by_patch[patch]


def pack(states):
    return pl.pallas_call(
        pack_kernel,
        grid=(REG_DEV, SHARE // HALF),
        in_specs=[pl.BlockSpec((1, HALF, SHARES, TILE_POINTS), lambda r, i: (r, i, 0, 0))],
        out_specs=pl.BlockSpec((SHARES, 1, HALF, TILE_POINTS), lambda r, i: (0, r, i, 0)),
        out_shape=pltpu.HBM((SHARES, REG_DEV, SHARE, TILE_POINTS), jnp.float32),
        cost_estimate=pl.CostEstimate(flops=0, bytes_accessed=8 << 20, transcendentals=0),
        name="pack",
    )(states)


def unpack_kernel(x_ref, *refs):
    o_ref = refs[-1]
    for number in range(TILE_POINTS // WIDTH):
        pieces = x_ref[:, :, columns(number)]
        by_patch = jnp.stack([pieces[PLACE[patch]] for patch in range(SHARES)])
        o_ref[0, :, :, columns(number)] = jnp.swapaxes(by_patch, 0, 1)


def unpack(pieces, region, target=None):
    extra = [] if target is None else [target]
    return pl.pallas_call(
        unpack_kernel,
        grid=(SHARE // HALF,),
        in_specs=[pl.BlockSpec((SHARES, HALF, TILE_POINTS), lambda i: (0, i, 0))]
        + [pl.BlockSpec(memory_space=pl.ANY)] * len(extra),
        out_specs=pl.BlockSpec((1, HALF, SHARES, TILE_POINTS), lambda i: (region, i, 0, 0)),
        out_shape=jax.ShapeDtypeStruct((REG_DEV, SHARE, SHARES, TILE_POINTS), jnp.float32),
        input_output_aliases={1: 0} if extra else {},
        cost_estimate=pl.CostEstimate(flops=0, bytes_accessed=4 << 20, transcendentals=0),
        name="unpack",
    )(pltpu.with_memory_space_constraint(pieces, pltpu.HBM), *extra)


def slot_of(area, place, cycle):
    ring = lax.rem(area // REG_DEV - place + 1 + cycle, cycle)
    return ring * REG_DEV + lax.rem(area, REG_DEV)


def area_of(block, row, neighbours):
    return row if block == 0 else neighbours[row, block - 1]


def analysis_kernel(
    cycle,
    place_ref,
    live_ref,
    nbr_ref,
    factor_ref,
    prev_near,
    prev_far,
    own_near,
    own_far,
    next_near,
    next_far,
    values_ref,
    precision_ref,
    lookup_ref,
    out_ref,
    pert,
    mean,
    scaled,
    root,
):
    place = place_ref[0]
    half = MEMBER_TOTAL // 2
    for ring, source in enumerate(
        ((prev_near, prev_far), (own_near, own_far), (next_near, next_far))
    ):
        for part in range(REG_DEV):
            slot = ring * REG_DEV + part
            blocks = [ref[:, part].reshape(half, NOBS) for ref in source]
            total = sum(jnp.sum(block, axis=0, keepdims=True) for block in blocks)
            average = total * (1.0 / MEMBER_TOTAL)
            for side, block in enumerate(blocks):
                pert[slot, pl.ds(side * half, half), :] = block - average
            mean[slot] = jnp.broadcast_to(average, (8, NOBS))
    slots = lax.broadcasted_iota(jnp.int32, (1, NOBS), 1)
    rows = lax.broadcasted_iota(jnp.int32, (MEMBER_TOTAL, MEMBER_TOTAL), 0)
    cols = lax.broadcasted_iota(jnp.int32, (MEMBER_TOTAL, MEMBER_TOTAL), 1)
    identity = jnp.where(rows == cols, 1.0, 0.0).astype(jnp.float32)
    drives, norms = [], []
    for region in range(REG_DEV):
        row = place * REG_DEV + region
        lookup = lookup_ref[region]
        taper = jnp.zeros(lookup.shape, jnp.float32)
        for level in range(LEVELS):
            taper = jnp.where(lookup == level, factor_ref[level], taper)
        gram = ((MEMBER_TOTAL - 1) / inflation) * identity
        drive = jnp.zeros((MEMBER_TOTAL, 128), jnp.float32)
        for block in range(NBR + 1):
            area = area_of(block, row, nbr_ref)
            slot = slot_of(area, place, cycle)
            weight = jnp.where(slots < live_ref[area], precision_ref[pl.ds(area, 1), :], 0.0)
            weight = weight * taper[block : block + 1, :]
            offset = values_ref[pl.ds(area, 1), :] - mean[slot][0:1, :]
            block_pert = pert[slot]
            gram = gram + dot_rows(block_pert * weight, block_pert)
            drive = drive + dot_rows(
                block_pert, jnp.broadcast_to(weight * offset, (128, NOBS))
            )
        norm = jnp.sqrt(jnp.sum(gram * gram, keepdims=True))
        first = gram / norm
        step = 1.5 * identity - 0.5 * first
        root[region] = step
        scaled[region] = dot(first, step)
        drives.append(drive)
        norms.append(norm)

    def sweep(_, carry):
        steps = [
            1.5 * identity - 0.5 * dot(root[region], scaled[region]) for region in range(REG_DEV)
        ]
        roots = [dot(steps[region], root[region]) for region in range(REG_DEV)]
        scales = [dot(scaled[region], steps[region]) for region in range(REG_DEV)]
        for region in range(REG_DEV):
            root[region] = roots[region]
            scaled[region] = scales[region]
        return carry

    lax.fori_loop(0, NSIT - 2, sweep, 0)
    for region in range(REG_DEV):
        root_mat = root[region]
        step = 1.5 * identity - 0.5 * dot(root_mat, scaled[region])
        root_mat = dot(step, root_mat)
        shift = dot(root_mat, dot(root_mat, drives[region])) / norms[region]
        factor = jnp.sqrt(jnp.float32(MEMBER_TOTAL - 1)) / jnp.sqrt(norms[region])
        out_ref[region] = factor * root_mat + jnp.concatenate([shift, shift], axis=1)


def analysis(cycle, place, live, nbr, factors, cells, values, precisions, lookup):
    whole = lambda *shape: pl.BlockSpec(shape, lambda i, *_: (0,) * len(shape))
    areas = values.shape[0]
    return pl.pallas_call(
        functools.partial(analysis_kernel, cycle),
        grid_spec=pltpu.PrefetchScalarGridSpec(
            num_scalar_prefetch=4,
            grid=(1,),
            in_specs=[whole(RINGS, REG_DEV, SHARE, NOBS)] * len(cells)
            + [
                whole(areas, NOBS),
                whole(areas, NOBS),
                pl.BlockSpec((REG_DEV, NBR + 1, NOBS), lambda i, p, *_: (p[0], 0, 0)),
            ],
            out_specs=whole(REG_DEV, MEMBER_TOTAL, MEMBER_TOTAL),
            scratch_shapes=[
                pltpu.VMEM((3 * REG_DEV, MEMBER_TOTAL, NOBS), jnp.float32),
                pltpu.VMEM((3 * REG_DEV, 8, NOBS), jnp.float32),
                pltpu.VMEM((REG_DEV, MEMBER_TOTAL, MEMBER_TOTAL), jnp.float32),
                pltpu.VMEM((REG_DEV, MEMBER_TOTAL, MEMBER_TOTAL), jnp.float32),
            ],
        ),
        out_shape=jax.ShapeDtypeStruct((REG_DEV, MEMBER_TOTAL, MEMBER_TOTAL), jnp.float32),
        compiler_params=pltpu.CompilerParams(vmem_limit_bytes=24 << 20),
        cost_estimate=pl.CostEstimate(
            flops=60 * 6 * 2 * 256**3, bytes_accessed=3 << 20, transcendentals=0
        ),
        name="analysis",
    )(place, live, nbr, factors, *cells, values, precisions, lookup)


def apply_kernel(
    cycle,
    region,
    place_ref,
    nbr_ref,
    factor_ref,
    blend_ref,
    order_ref,
    prev_ref,
    own_ref,
    next_ref,
    x_ref,
    o_ref,
    mix,
    cells,
):
    @pl.when(pl.program_id(0) == 0)
    def _():
        place = place_ref[0]
        row = place * REG_DEV + region
        shares = [jnp.float32(0.0)] * (3 * REG_DEV)
        total = jnp.float32(0.0)
        for block in range(NBR + 1):
            slot = slot_of(area_of(block, row, nbr_ref), place, cycle)
            value = factor_ref[blend_ref[region, 0, block]]
            total = total + value
            shares = [s + jnp.where(slot == k, value, 0.0) for k, s in enumerate(shares)]
        acc = jnp.zeros((MEMBER_TOTAL, MEMBER_TOTAL), jnp.float32)
        for ring, source in enumerate((prev_ref, own_ref, next_ref)):
            for part in range(REG_DEV):
                acc = acc + shares[ring * REG_DEV + part] * source[part]
        mix[...] = (acc / total).T

    here = pl.ds(pl.multiple_of(pl.program_id(0) * WIDTH, WIDTH), WIDTH)
    for rank in range(SHARES):
        cells[pl.ds(rank * SHARE, SHARE), :] = x_ref[order_ref[rank], region, :, here]
    states = cells[...]
    center = jnp.sum(states, axis=0, keepdims=True) * (1.0 / MEMBER_TOTAL)
    updated = center + dot(mix[...], states - center)
    for rank in range(SHARES):
        o_ref[order_ref[rank]] = updated[rank * SHARE : (rank + 1) * SHARE, :]


def apply(cycle, region, scalars, beside, states):
    matrix = pl.BlockSpec(
        (REG_DEV, MEMBER_TOTAL, MEMBER_TOTAL), lambda i: (0, 0, 0), pipeline_mode=pl.Buffered(1)
    )
    return pl.pallas_call(
        functools.partial(apply_kernel, cycle, region),
        grid=(TILE_POINTS // WIDTH,),
        in_specs=[SMEM] * 5 + [matrix] * 3 + [pl.BlockSpec(memory_space=pltpu.VMEM)],
        out_specs=pl.BlockSpec((SHARES, SHARE, WIDTH), lambda i: (0, 0, i)),
        out_shape=pltpu.HBM((SHARES, SHARE, TILE_POINTS), jnp.float32),
        scratch_shapes=[
            pltpu.VMEM((MEMBER_TOTAL, MEMBER_TOTAL), jnp.float32),
            pltpu.VMEM((MEMBER_TOTAL, WIDTH), jnp.float32),
        ],
        compiler_params=pltpu.CompilerParams(vmem_limit_bytes=24 << 20),
        cost_estimate=pl.CostEstimate(
            flops=6 * 2 * 256 * 256 * TILE_POINTS, bytes_accessed=5 << 20, transcendentals=0
        ),
        name="apply",
    )(*scalars, *beside, pltpu.with_memory_space_constraint(states, pltpu.VMEM))


def member_at(index, along_x, along_z):
    columns = SHARES // RINGS
    return (index // RINGS + along_x) % columns * RINGS + (index + along_z) % RINGS


RING_ORDER = (0, 4, 1, 5, 2, 6, 7, 3)


def traded(pieces):
    return lax.all_to_all(pieces, "member", 0, 0, axis_index_groups=[LISTED], tiled=True)


def from_ring(cells):
    def sent(piece, step):
        return lax.ppermute(
            piece, "member", [(i, member_at(i, 0, step)) for i in range(SHARES)]
        )

    pair = jnp.stack([cells, sent(cells, 4)])
    return jnp.concatenate([pair] + [sent(pair, step) for step in (1, 2, 7)])


def from_around(near):
    count = lax.axis_size("region")
    got = []
    for shift in (1, 0, -1):
        for across in (0, 1):
            if shift == 0 and across == 0:
                got.append(near)
                continue
            pairs = [
                (g * SHARES + i, (g + shift) % count * SHARES + member_at(i, across, 0))
                for g in range(count)
                for i in range(SHARES)
            ]
            got.append(lax.ppermute(near, ("region", "member"), pairs))
    return got


def from_beside(cells):
    count = lax.axis_size("region")
    before = lax.ppermute(cells, "region", [(i, (i + 1) % count) for i in range(count)])
    after = lax.ppermute(cells, "region", [((i + 1) % count, i) for i in range(count)])
    return before, after


def body(
    prior_states,
    prior_in_sensor_space,
    sensor_readings,
    error_precisions,
    live_tallies,
    adjacent_areas,
    taper_lookup,
    blend_lookup,
    taper_factors,
):
    cycle = lax.axis_size("region")
    place = lax.axis_index("region").astype(jnp.int32)[None]
    index = lax.axis_index("member").astype(jnp.int32)
    order = jnp.stack(
        [member_at(index, across, -step) for across in (0, 1) for step in RING_ORDER]
    )
    order = jnp.take(jnp.array(PLACE, jnp.int32), order)
    near = from_ring(prior_in_sensor_space)
    packed = pack(prior_states)
    packed, near = lax.optimization_barrier((packed, near))
    cells = from_around(near)
    states = traded(packed)
    transforms = analysis(
        cycle,
        place,
        live_tallies,
        adjacent_areas,
        taper_factors,
        cells,
        sensor_readings,
        error_precisions,
        taper_lookup,
    )
    left, right = from_beside(transforms)
    scalars = (place, adjacent_areas, taper_factors, blend_lookup, order)
    beside = (left, transforms, right)
    out = None
    for region in range(REG_DEV):
        updated = apply(cycle, region, scalars, beside, states)
        out = unpack(traded(updated), region, out)
    return out


def solution(mesh):
    placed = (
        P("region", "member", None, None),
        P("region", "member", None),
        P(),
        P(),
        P(),
        P(),
        P(),
        P("region", "member", None),
        P(),
    )
    return jax.shard_map(
        body,
        mesh=mesh,
        in_specs=placed,
        out_specs=P("region", "member", None, None),
        check_vma=False,
    )
```

```python
import functools

import jax
import jax.numpy as jnp
from jax import lax
from jax.experimental import pallas as pl
from jax.experimental.pallas import tpu as pltpu
from jax.sharding import PartitionSpec as P

MEMBER_TOTAL = 256
NOBS = 256
NBR = 4
NSIT = 8
REG_DEV = 2
LEVELS = 16
TILE_POINTS = 2048
SHARES = 16
SHARE = 16
RINGS = 8

inflation = 1.1
highest = lax.Precision.HIGHEST
SMEM = pl.BlockSpec(memory_space=pltpu.SMEM)


def dot(a, b):
    return lax.dot_general(
        a, b, (((1,), (0,)), ((), ())), precision=highest, preferred_element_type=jnp.float32
    )


def dot_rows(a, b):
    return lax.dot_general(
        a, b, (((1,), (1,)), ((), ())), precision=highest, preferred_element_type=jnp.float32
    )


WIDTH = 512
SIDES = SHARES // RINGS

LISTED = [0, 2, 5, 1, 7, 4, 3, 6]
ALL_LISTED = [0, 7, 1, 6, 2, 5, 3, 4, 12, 11, 13, 10, 14, 9, 15, 8]
HALF = SHARE // 2


def columns(number):
    return pl.ds(number * WIDTH, WIDTH)


def pack_kernel(x_ref, *refs):
    o_ref = refs[-1]
    for number in range(TILE_POINTS // WIDTH):
        by_patch = jnp.swapaxes(x_ref[0, :, :, columns(number)], 0, 1)
        for place, patch in enumerate(ALL_LISTED):
            o_ref[place, 0, :, columns(number)] = by_patch[patch]


def pack(states, region, target=None):
    extra = [] if target is None else [target]
    return pl.pallas_call(
        pack_kernel,
        grid=(SHARE // HALF,),
        in_specs=[pl.BlockSpec((1, HALF, SHARES, TILE_POINTS), lambda i: (region, i, 0, 0))]
        + [pl.BlockSpec(memory_space=pl.ANY)] * len(extra),
        out_specs=pl.BlockSpec((SHARES, 1, HALF, TILE_POINTS), lambda i: (0, region, i, 0)),
        out_shape=pltpu.HBM((SHARES, REG_DEV, SHARE, TILE_POINTS), jnp.float32),
        input_output_aliases={1: 0} if extra else {},
        cost_estimate=pl.CostEstimate(flops=0, bytes_accessed=4 << 20, transcendentals=0),
        name="pack",
    )(states, *extra)


def unpack_kernel(_, x_ref, *refs):
    o_ref = refs[-1]
    for number in range(TILE_POINTS // WIDTH):
        pieces = x_ref[:, 0, :, columns(number)]
        by_patch = jnp.stack([pieces[LISTED.index(patch)] for patch in range(RINGS)])
        o_ref[0, :, :, columns(number)] = jnp.swapaxes(by_patch, 0, 1)


def unpack(region, sides, pieces, target=None):
    extra = [] if target is None else [target]
    return pl.pallas_call(
        unpack_kernel,
        grid_spec=pltpu.PrefetchScalarGridSpec(
            num_scalar_prefetch=1,
            grid=sides.shape,
            in_specs=[
                pl.BlockSpec((RINGS, 1, SHARE, TILE_POINTS), lambda k, sides: (0, k, 0, 0))
            ]
            + [pl.BlockSpec(memory_space=pl.ANY)] * len(extra),
            out_specs=pl.BlockSpec(
                (1, SHARE, RINGS, TILE_POINTS), lambda k, sides: (region, 0, sides[k], 0)
            ),
        ),
        out_shape=jax.ShapeDtypeStruct((REG_DEV, SHARE, SHARES, TILE_POINTS), jnp.float32),
        input_output_aliases={2: 0} if extra else {},
        cost_estimate=pl.CostEstimate(flops=0, bytes_accessed=4 << 20, transcendentals=0),
        name="unpack",
    )(sides, pltpu.with_memory_space_constraint(pieces, pltpu.HBM), *extra)


def slot_of(area, place, cycle):
    ring = lax.rem(area // REG_DEV - place + 1 + cycle, cycle)
    return ring * REG_DEV + lax.rem(area, REG_DEV)


def area_of(block, row, neighbours):
    return row if block == 0 else neighbours[row, block - 1]


EXTRA = 8


def analysis_kernel(
    cycle,
    place_ref,
    live_ref,
    nbr_ref,
    factor_ref,
    prev_near,
    prev_far,
    own_near,
    own_far,
    next_near,
    next_far,
    values_ref,
    precision_ref,
    lookup_ref,
    out_ref,
    pert,
    mean,
    scaled,
    root,
):
    place = place_ref[0]
    half = MEMBER_TOTAL // 2
    for ring, source in enumerate(
        ((prev_near, prev_far), (own_near, own_far), (next_near, next_far))
    ):
        for part in range(REG_DEV):
            slot = ring * REG_DEV + part
            blocks = [ref[:, part].reshape(half, NOBS) for ref in source]
            total = sum(jnp.sum(block, axis=0, keepdims=True) for block in blocks)
            average = total * (1.0 / MEMBER_TOTAL)
            for side, block in enumerate(blocks):
                pert[slot, pl.ds(side * half, half), :] = block - average
            mean[slot] = jnp.broadcast_to(average, (8, NOBS))
    slots = lax.broadcasted_iota(jnp.int32, (1, NOBS), 1)
    rows = lax.broadcasted_iota(jnp.int32, (MEMBER_TOTAL, MEMBER_TOTAL), 0)
    cols = lax.broadcasted_iota(jnp.int32, (MEMBER_TOTAL, MEMBER_TOTAL), 1)
    identity = jnp.where(rows == cols, 1.0, 0.0).astype(jnp.float32)
    drives, norms = [], []
    for region in range(REG_DEV):
        row = place * REG_DEV + region
        lookup = lookup_ref[region]
        taper = jnp.zeros(lookup.shape, jnp.float32)
        for level in range(LEVELS):
            taper = jnp.where(lookup == level, factor_ref[level], taper)
        gram = ((MEMBER_TOTAL - 1) / inflation) * identity
        drive = jnp.zeros((MEMBER_TOTAL, 128), jnp.float32)
        for block in range(NBR + 1):
            area = area_of(block, row, nbr_ref)
            slot = slot_of(area, place, cycle)
            weight = jnp.where(slots < live_ref[area], precision_ref[pl.ds(area, 1), :], 0.0)
            weight = weight * taper[block : block + 1, :]
            offset = values_ref[pl.ds(area, 1), :] - mean[slot][0:1, :]
            block_pert = pert[slot]
            gram = gram + dot_rows(block_pert * weight, block_pert)
            drive = drive + dot_rows(
                block_pert, jnp.broadcast_to(weight * offset, (128, NOBS))
            )
        norm = jnp.sqrt(jnp.sum(gram * gram, keepdims=True))
        first = gram / norm
        step = 1.5 * identity - 0.5 * first
        root[region] = step
        scaled[region] = dot(first, step)
        drives.append(drive)
        norms.append(norm)

    def sweep(_, carry):
        steps = [
            1.5 * identity - 0.5 * dot(root[region], scaled[region]) for region in range(REG_DEV)
        ]
        roots = [dot(steps[region], root[region]) for region in range(REG_DEV)]
        scales = [dot(scaled[region], steps[region]) for region in range(REG_DEV)]
        for region in range(REG_DEV):
            root[region] = roots[region]
            scaled[region] = scales[region]
        return carry

    lax.fori_loop(0, NSIT - 2, sweep, 0)
    roots, extra = [], []
    for region in range(REG_DEV):
        root_mat = root[region]
        step = 1.5 * identity - 0.5 * dot(root_mat, scaled[region])
        root_mat = dot(step, root_mat)
        shift = dot(root_mat, dot(root_mat, drives[region])) / norms[region]
        factor = jnp.sqrt(jnp.float32(MEMBER_TOTAL - 1)) / jnp.sqrt(norms[region])
        roots.append(factor * root_mat)
        extra.append(shift.T[0:1, :])
    out_ref[pl.ds(0, MEMBER_TOTAL), :] = jnp.where(rows <= cols, roots[0], roots[1])
    diagonal = jnp.sum(roots[1] * identity, axis=0, keepdims=True)
    blank = jnp.zeros((EXTRA - 3, MEMBER_TOTAL), jnp.float32)
    out_ref[pl.ds(MEMBER_TOTAL, EXTRA), :] = jnp.concatenate([*extra, diagonal, blank])


def analysis(cycle, place, live, nbr, factors, cells, values, precisions, lookup):
    whole = lambda *shape: pl.BlockSpec(shape, lambda i, *_: (0,) * len(shape))
    areas = values.shape[0]
    return pl.pallas_call(
        functools.partial(analysis_kernel, cycle),
        grid_spec=pltpu.PrefetchScalarGridSpec(
            num_scalar_prefetch=4,
            grid=(1,),
            in_specs=[whole(RINGS, REG_DEV, SHARE, NOBS)] * len(cells)
            + [
                whole(areas, NOBS),
                whole(areas, NOBS),
                pl.BlockSpec((REG_DEV, NBR + 1, NOBS), lambda i, p, *_: (p[0], 0, 0)),
            ],
            out_specs=whole(MEMBER_TOTAL + EXTRA, MEMBER_TOTAL),
            scratch_shapes=[
                pltpu.VMEM((3 * REG_DEV, MEMBER_TOTAL, NOBS), jnp.float32),
                pltpu.VMEM((3 * REG_DEV, 8, NOBS), jnp.float32),
                pltpu.VMEM((REG_DEV, MEMBER_TOTAL, MEMBER_TOTAL), jnp.float32),
                pltpu.VMEM((REG_DEV, MEMBER_TOTAL, MEMBER_TOTAL), jnp.float32),
            ],
        ),
        out_shape=jax.ShapeDtypeStruct((MEMBER_TOTAL + EXTRA, MEMBER_TOTAL), jnp.float32),
        compiler_params=pltpu.CompilerParams(vmem_limit_bytes=24 << 20),
        cost_estimate=pl.CostEstimate(
            flops=60 * 6 * 2 * 256**3, bytes_accessed=3 << 20, transcendentals=0
        ),
        name="analysis",
    )(place, live, nbr, factors, *cells, values, precisions, lookup)


def blend_kernel(
    cycle,
    place_ref,
    nbr_ref,
    factor_ref,
    blend_ref,
    enter_ref,
    leave_ref,
    prev_ref,
    own_ref,
    next_ref,
    o_ref,
):
    place = place_ref[0]
    rows = lax.broadcasted_iota(jnp.int32, (MEMBER_TOTAL, MEMBER_TOTAL), 0)
    cols = lax.broadcasted_iota(jnp.int32, (MEMBER_TOTAL, MEMBER_TOTAL), 1)
    for region in range(REG_DEV):
        row = place * REG_DEV + region
        shares = [jnp.float32(0.0)] * (3 * REG_DEV)
        total = jnp.float32(0.0)
        for block in range(NBR + 1):
            slot = slot_of(area_of(block, row, nbr_ref), place, cycle)
            value = factor_ref[blend_ref[region, 0, block]]
            total = total + value
            shares = [s + jnp.where(slot == k, value, 0.0) for k, s in enumerate(shares)]
        square = pl.ds(0, MEMBER_TOTAL)
        upper = jnp.zeros((MEMBER_TOTAL, MEMBER_TOTAL), jnp.float32)
        lower = upper
        shift = jnp.zeros((1, MEMBER_TOTAL), jnp.float32)
        diagonal = shift
        for ring, source in enumerate((prev_ref, own_ref, next_ref)):
            first, second = shares[ring * REG_DEV : (ring + 1) * REG_DEV]
            upper = upper + first * source[square, :]
            lower = lower + second * source[square, :]
            below = source[pl.ds(MEMBER_TOTAL, EXTRA), :]
            shift = shift + first * below[0:1, :] + second * below[1:2, :]
            diagonal = diagonal + second * below[2:3, :]
        joined = jnp.where(rows <= cols, upper, lower)
        mirrored = jnp.where(rows == cols, diagonal, joined.T)
        mixed = ((joined + mirrored + shift) / total).T
        for order_ref in (enter_ref, leave_ref):
            for rank in range(SHARES):
                first = pl.multiple_of(order_ref[rank] * SHARE, SHARE)
                o_ref[region, pl.ds(first, SHARE), :] = mixed[rank * SHARE : (rank + 1) * SHARE, :]
            if order_ref is enter_ref:
                mixed = o_ref[region].T


def blend(cycle, scalars, beside):
    return pl.pallas_call(
        functools.partial(blend_kernel, cycle),
        in_specs=[SMEM] * 6 + [pl.BlockSpec(memory_space=pltpu.VMEM)] * 3,
        out_specs=pl.BlockSpec(memory_space=pltpu.VMEM),
        out_shape=jax.ShapeDtypeStruct((REG_DEV, MEMBER_TOTAL, MEMBER_TOTAL), jnp.float32),
        compiler_params=pltpu.CompilerParams(vmem_limit_bytes=24 << 20),
        cost_estimate=pl.CostEstimate(
            flops=24 * 256 * 256, bytes_accessed=2 << 20, transcendentals=0
        ),
        name="blend",
    )(*scalars, *beside)


def apply_kernel(mix_ref, x_ref, *o_refs):
    half = MEMBER_TOTAL // SIDES
    states = x_ref[:, 0].reshape(MEMBER_TOTAL, WIDTH)
    center = jnp.sum(states, axis=0, keepdims=True) * (1.0 / MEMBER_TOTAL)
    updated = center + dot(mix_ref[0], states - center)
    for side in range(SIDES):
        part = updated[side * half : (side + 1) * half].reshape(RINGS, SHARE, WIDTH)
        if len(o_refs) == 1:
            o_refs[0][:, side] = part
        else:
            o_refs[side][:, 0] = part


def apply(mixed, region, states, arrays):
    sides = SIDES // arrays
    return pl.pallas_call(
        apply_kernel,
        grid=(TILE_POINTS // WIDTH,),
        in_specs=[
            pl.BlockSpec((1, MEMBER_TOTAL, MEMBER_TOTAL), lambda i: (region, 0, 0)),
            pl.BlockSpec((SHARES, 1, SHARE, WIDTH), lambda i: (0, region, 0, i)),
        ],
        out_specs=[pl.BlockSpec((RINGS, sides, SHARE, WIDTH), lambda i: (0, 0, 0, i))] * arrays,
        out_shape=[pltpu.HBM((RINGS, sides, SHARE, TILE_POINTS), jnp.float32)] * arrays,
        compiler_params=pltpu.CompilerParams(vmem_limit_bytes=24 << 20),
        cost_estimate=pl.CostEstimate(
            flops=6 * 2 * 256 * 256 * TILE_POINTS, bytes_accessed=5 << 20, transcendentals=0
        ),
        name="apply",
    )(mixed, pltpu.with_memory_space_constraint(states, pltpu.HBM))


def member_at(index, along_x, along_z):
    columns = SHARES // RINGS
    return (index // RINGS + along_x) % columns * RINGS + (index + along_z) % RINGS


RING_ORDER = (0, 4, 1, 5, 2, 6, 7, 3)


def listed_at(members, listed):
    place = jnp.zeros(members.shape, jnp.int32)
    for number, member in enumerate(listed):
        place = jnp.where(members == member, number, place)
    return place


def traded_by_all(pieces):
    return lax.all_to_all(pieces, "member", 0, 0, axis_index_groups=[ALL_LISTED], tiled=True)


def traded(pieces):
    groups = [[side * RINGS + along for along in LISTED] for side in range(SIDES)]
    return lax.all_to_all(pieces, "member", 0, 0, axis_index_groups=groups, tiled=True)


def across(pieces):
    return lax.ppermute(pieces, "member", [(i, member_at(i, 1, 0)) for i in range(SHARES)])


def from_ring(cells, states):
    def sent(piece, step):
        return lax.ppermute(
            piece, "member", [(i, member_at(i, 0, step)) for i in range(SHARES)]
        )

    pair = jnp.stack([cells, sent(cells, 4)])
    packed, pair = lax.optimization_barrier((pack(states, 0), pair))
    packed = pack(states, 1, packed)
    pieces = [sent(pair, step) for step in (1, 2, 7)]
    packed, pieces = lax.optimization_barrier((packed, pieces))
    return jnp.concatenate([pair] + pieces), packed


def from_around(near):
    count = lax.axis_size("region")
    got = []
    for shift in (1, 0, -1):
        for across in (0, 1):
            if shift == 0 and across == 0:
                got.append(near)
                continue
            pairs = [
                (g * SHARES + i, (g + shift) % count * SHARES + member_at(i, across, 0))
                for g in range(count)
                for i in range(SHARES)
            ]
            got.append(lax.ppermute(near, ("region", "member"), pairs))
    return got


def from_beside(cells):
    count = lax.axis_size("region")
    before = lax.ppermute(cells, "region", [(i, (i + 1) % count) for i in range(count)])
    after = lax.ppermute(cells, "region", [((i + 1) % count, i) for i in range(count)])
    return before, after


def body(
    prior_states,
    prior_in_sensor_space,
    sensor_readings,
    error_precisions,
    live_tallies,
    adjacent_areas,
    taper_lookup,
    blend_lookup,
    taper_factors,
):
    cycle = lax.axis_size("region")
    place = lax.axis_index("region").astype(jnp.int32)[None]
    index = lax.axis_index("member").astype(jnp.int32)
    along = (index % RINGS - jnp.array(RING_ORDER, jnp.int32)) % RINGS
    here = index // RINGS
    leave = listed_at(along, LISTED)
    leave = jnp.concatenate([leave, RINGS + leave])
    enter = jnp.concatenate([here * RINGS + along, (1 - here) * RINGS + along])
    enter = listed_at(enter, ALL_LISTED)
    here, there = here[None], 1 - here[None]
    near, packed = from_ring(prior_in_sensor_space, prior_states)
    cells = from_around(near)
    states = traded_by_all(packed)
    transforms = analysis(
        cycle,
        place,
        live_tallies,
        adjacent_areas,
        taper_factors,
        cells,
        sensor_readings,
        error_precisions,
        taper_lookup,
    )
    left, right = from_beside(transforms)
    scalars = (place, adjacent_areas, taper_factors, blend_lookup, enter, leave)
    mixed = blend(cycle, scalars, (left, transforms, right))
    (leaving,) = apply(mixed, 0, states, 1)
    first = traded(leaving)
    near, far = apply(mixed, 1, states, 2)
    both = jnp.concatenate([near, across(far)], axis=1)
    both, first = lax.optimization_barrier((both, first))
    second = traded(both)
    out = unpack(0, here, first)
    out = unpack(0, there, across(first[:, 1:]), out)
    return unpack(1, jnp.concatenate([here, there]), second, out)


def solution(mesh):
    placed = (
        P("region", "member", None, None),
        P("region", "member", None),
        P(),
        P(),
        P(),
        P(),
        P(),
        P("region", "member", None),
        P(),
    )
    return jax.shard_map(
        body,
        mesh=mesh,
        in_specs=placed,
        out_specs=P("region", "member", None, None),
        check_vma=False,
    )
```

```python
import functools

import jax
import jax.numpy as jnp
from jax import lax
from jax.experimental import pallas as pl
from jax.experimental.pallas import tpu as pltpu
from jax.sharding import PartitionSpec as P

MEMBER_TOTAL = 256
NOBS = 256
NBR = 4
NSIT = 8
REG_DEV = 2
LEVELS = 16
TILE_POINTS = 2048
SHARES = 16
SHARE = 16
RINGS = 8

inflation = 1.1
highest = lax.Precision.HIGHEST
SMEM = pl.BlockSpec(memory_space=pltpu.SMEM)


def dot(a, b):
    return lax.dot_general(
        a, b, (((1,), (0,)), ((), ())), precision=highest, preferred_element_type=jnp.float32
    )


def dot_rows(a, b):
    return lax.dot_general(
        a, b, (((1,), (1,)), ((), ())), precision=highest, preferred_element_type=jnp.float32
    )


WIDTH = 512
SIDES = SHARES // RINGS

LISTED = [0, 4, 1, 5, 2, 6, 3, 7]
ALL_LISTED = [0, 3, 6, 1, 4, 7, 2, 5, 8, 11, 14, 9, 12, 15, 10, 13]
HALF = SHARE // 2


def columns(number):
    return pl.ds(number * WIDTH, WIDTH)


def pack_kernel(x_ref, *refs):
    o_ref = refs[-1]
    for number in range(TILE_POINTS // WIDTH):
        by_patch = jnp.swapaxes(x_ref[0, :, :, columns(number)], 0, 1)
        for place, patch in enumerate(ALL_LISTED):
            o_ref[place, 0, :, columns(number)] = by_patch[patch]


def pack(states, region, target=None):
    extra = [] if target is None else [target]
    return pl.pallas_call(
        pack_kernel,
        grid=(SHARE // HALF,),
        in_specs=[pl.BlockSpec((1, HALF, SHARES, TILE_POINTS), lambda i: (region, i, 0, 0))]
        + [pl.BlockSpec(memory_space=pl.ANY)] * len(extra),
        out_specs=pl.BlockSpec((SHARES, 1, HALF, TILE_POINTS), lambda i: (0, region, i, 0)),
        out_shape=pltpu.HBM((SHARES, REG_DEV, SHARE, TILE_POINTS), jnp.float32),
        input_output_aliases={1: 0} if extra else {},
        cost_estimate=pl.CostEstimate(flops=0, bytes_accessed=4 << 20, transcendentals=0),
        name="pack",
    )(states, *extra)


def unpack_kernel(_, x_ref, *refs):
    o_ref = refs[-1]
    for number in range(TILE_POINTS // WIDTH):
        pieces = x_ref[:, 0, :, columns(number)]
        by_patch = jnp.stack([pieces[LISTED.index(patch)] for patch in range(RINGS)])
        o_ref[0, :, :, columns(number)] = jnp.swapaxes(by_patch, 0, 1)


def unpack(region, sides, pieces, target=None):
    extra = [] if target is None else [target]
    return pl.pallas_call(
        unpack_kernel,
        grid_spec=pltpu.PrefetchScalarGridSpec(
            num_scalar_prefetch=1,
            grid=sides.shape,
            in_specs=[
                pl.BlockSpec((RINGS, 1, SHARE, TILE_POINTS), lambda k, sides: (0, k, 0, 0))
            ]
            + [pl.BlockSpec(memory_space=pl.ANY)] * len(extra),
            out_specs=pl.BlockSpec(
                (1, SHARE, RINGS, TILE_POINTS), lambda k, sides: (region, 0, sides[k], 0)
            ),
        ),
        out_shape=jax.ShapeDtypeStruct((REG_DEV, SHARE, SHARES, TILE_POINTS), jnp.float32),
        input_output_aliases={2: 0} if extra else {},
        cost_estimate=pl.CostEstimate(flops=0, bytes_accessed=4 << 20, transcendentals=0),
        name="unpack",
    )(sides, pltpu.with_memory_space_constraint(pieces, pltpu.HBM), *extra)


def slot_of(area, place, cycle):
    ring = lax.rem(area // REG_DEV - place + 1 + cycle, cycle)
    return ring * REG_DEV + lax.rem(area, REG_DEV)


def area_of(block, row, neighbours):
    return row if block == 0 else neighbours[row, block - 1]


EXTRA = 8


def analysis_kernel(
    cycle,
    place_ref,
    live_ref,
    nbr_ref,
    factor_ref,
    prev_near,
    prev_far,
    own_near,
    own_far,
    next_near,
    next_far,
    values_ref,
    precision_ref,
    lookup_ref,
    out_ref,
    pert,
    mean,
    scaled,
    root,
):
    place = place_ref[0]
    half = MEMBER_TOTAL // 2
    for ring, source in enumerate(
        ((prev_near, prev_far), (own_near, own_far), (next_near, next_far))
    ):
        for part in range(REG_DEV):
            slot = ring * REG_DEV + part
            blocks = [ref[:, part].reshape(half, NOBS) for ref in source]
            total = sum(jnp.sum(block, axis=0, keepdims=True) for block in blocks)
            average = total * (1.0 / MEMBER_TOTAL)
            for side, block in enumerate(blocks):
                pert[slot, pl.ds(side * half, half), :] = block - average
            mean[slot] = jnp.broadcast_to(average, (8, NOBS))
    slots = lax.broadcasted_iota(jnp.int32, (1, NOBS), 1)
    rows = lax.broadcasted_iota(jnp.int32, (MEMBER_TOTAL, MEMBER_TOTAL), 0)
    cols = lax.broadcasted_iota(jnp.int32, (MEMBER_TOTAL, MEMBER_TOTAL), 1)
    identity = jnp.where(rows == cols, 1.0, 0.0).astype(jnp.float32)
    drives, norms = [], []
    for region in range(REG_DEV):
        row = place * REG_DEV + region
        lookup = lookup_ref[region]
        taper = jnp.zeros(lookup.shape, jnp.float32)
        for level in range(LEVELS):
            taper = jnp.where(lookup == level, factor_ref[level], taper)
        gram = ((MEMBER_TOTAL - 1) / inflation) * identity
        drive = jnp.zeros((MEMBER_TOTAL, 128), jnp.float32)
        for block in range(NBR + 1):
            area = area_of(block, row, nbr_ref)
            slot = slot_of(area, place, cycle)
            weight = jnp.where(slots < live_ref[area], precision_ref[pl.ds(area, 1), :], 0.0)
            weight = weight * taper[block : block + 1, :]
            offset = values_ref[pl.ds(area, 1), :] - mean[slot][0:1, :]
            block_pert = pert[slot]
            gram = gram + dot_rows(block_pert * weight, block_pert)
            drive = drive + dot_rows(
                block_pert, jnp.broadcast_to(weight * offset, (128, NOBS))
            )
        norm = jnp.sqrt(jnp.sum(gram * gram, keepdims=True))
        first = gram / norm
        step = 1.5 * identity - 0.5 * first
        root[region] = step
        scaled[region] = dot(first, step)
        drives.append(drive)
        norms.append(norm)

    def sweep(_, carry):
        steps = [
            1.5 * identity - 0.5 * dot(root[region], scaled[region]) for region in range(REG_DEV)
        ]
        roots = [dot(steps[region], root[region]) for region in range(REG_DEV)]
        scales = [dot(scaled[region], steps[region]) for region in range(REG_DEV)]
        for region in range(REG_DEV):
            root[region] = roots[region]
            scaled[region] = scales[region]
        return carry

    lax.fori_loop(0, NSIT - 2, sweep, 0)
    roots, extra = [], []
    for region in range(REG_DEV):
        root_mat = root[region]
        step = 1.5 * identity - 0.5 * dot(root_mat, scaled[region])
        root_mat = dot(step, root_mat)
        shift = dot(root_mat, dot(root_mat, drives[region])) / norms[region]
        factor = jnp.sqrt(jnp.float32(MEMBER_TOTAL - 1)) / jnp.sqrt(norms[region])
        roots.append(factor * root_mat)
        extra.append(shift.T[0:1, :])
    out_ref[pl.ds(0, MEMBER_TOTAL), :] = jnp.where(rows <= cols, roots[0], roots[1])
    diagonal = jnp.sum(roots[1] * identity, axis=0, keepdims=True)
    blank = jnp.zeros((EXTRA - 3, MEMBER_TOTAL), jnp.float32)
    out_ref[pl.ds(MEMBER_TOTAL, EXTRA), :] = jnp.concatenate([*extra, diagonal, blank])


def analysis(cycle, place, live, nbr, factors, cells, values, precisions, lookup):
    whole = lambda *shape: pl.BlockSpec(shape, lambda i, *_: (0,) * len(shape))
    areas = values.shape[0]
    return pl.pallas_call(
        functools.partial(analysis_kernel, cycle),
        grid_spec=pltpu.PrefetchScalarGridSpec(
            num_scalar_prefetch=4,
            grid=(1,),
            in_specs=[whole(RINGS, REG_DEV, SHARE, NOBS)] * len(cells)
            + [
                whole(areas, NOBS),
                whole(areas, NOBS),
                pl.BlockSpec((REG_DEV, NBR + 1, NOBS), lambda i, p, *_: (p[0], 0, 0)),
            ],
            out_specs=whole(MEMBER_TOTAL + EXTRA, MEMBER_TOTAL),
            scratch_shapes=[
                pltpu.VMEM((3 * REG_DEV, MEMBER_TOTAL, NOBS), jnp.float32),
                pltpu.VMEM((3 * REG_DEV, 8, NOBS), jnp.float32),
                pltpu.VMEM((REG_DEV, MEMBER_TOTAL, MEMBER_TOTAL), jnp.float32),
                pltpu.VMEM((REG_DEV, MEMBER_TOTAL, MEMBER_TOTAL), jnp.float32),
            ],
        ),
        out_shape=jax.ShapeDtypeStruct((MEMBER_TOTAL + EXTRA, MEMBER_TOTAL), jnp.float32),
        compiler_params=pltpu.CompilerParams(vmem_limit_bytes=24 << 20),
        cost_estimate=pl.CostEstimate(
            flops=60 * 6 * 2 * 256**3, bytes_accessed=3 << 20, transcendentals=0
        ),
        name="analysis",
    )(place, live, nbr, factors, *cells, values, precisions, lookup)


def blend_kernel(
    cycle,
    place_ref,
    nbr_ref,
    factor_ref,
    blend_ref,
    enter_ref,
    leave_ref,
    prev_ref,
    own_ref,
    next_ref,
    o_ref,
):
    place = place_ref[0]
    rows = lax.broadcasted_iota(jnp.int32, (MEMBER_TOTAL, MEMBER_TOTAL), 0)
    cols = lax.broadcasted_iota(jnp.int32, (MEMBER_TOTAL, MEMBER_TOTAL), 1)
    for region in range(REG_DEV):
        row = place * REG_DEV + region
        shares = [jnp.float32(0.0)] * (3 * REG_DEV)
        total = jnp.float32(0.0)
        for block in range(NBR + 1):
            slot = slot_of(area_of(block, row, nbr_ref), place, cycle)
            value = factor_ref[blend_ref[region, 0, block]]
            total = total + value
            shares = [s + jnp.where(slot == k, value, 0.0) for k, s in enumerate(shares)]
        square = pl.ds(0, MEMBER_TOTAL)
        upper = jnp.zeros((MEMBER_TOTAL, MEMBER_TOTAL), jnp.float32)
        lower = upper
        shift = jnp.zeros((1, MEMBER_TOTAL), jnp.float32)
        diagonal = shift
        for ring, source in enumerate((prev_ref, own_ref, next_ref)):
            first, second = shares[ring * REG_DEV : (ring + 1) * REG_DEV]
            upper = upper + first * source[square, :]
            lower = lower + second * source[square, :]
            below = source[pl.ds(MEMBER_TOTAL, EXTRA), :]
            shift = shift + first * below[0:1, :] + second * below[1:2, :]
            diagonal = diagonal + second * below[2:3, :]
        joined = jnp.where(rows <= cols, upper, lower)
        mirrored = jnp.where(rows == cols, diagonal, joined.T)
        mixed = ((joined + mirrored + shift) / total).T
        for order_ref in (enter_ref, leave_ref):
            for rank in range(SHARES):
                first = pl.multiple_of(order_ref[rank] * SHARE, SHARE)
                o_ref[region, pl.ds(first, SHARE), :] = mixed[rank * SHARE : (rank + 1) * SHARE, :]
            if order_ref is enter_ref:
                mixed = o_ref[region].T


def blend(cycle, scalars, beside):
    return pl.pallas_call(
        functools.partial(blend_kernel, cycle),
        in_specs=[SMEM] * 6 + [pl.BlockSpec(memory_space=pltpu.VMEM)] * 3,
        out_specs=pl.BlockSpec(memory_space=pltpu.VMEM),
        out_shape=jax.ShapeDtypeStruct((REG_DEV, MEMBER_TOTAL, MEMBER_TOTAL), jnp.float32),
        compiler_params=pltpu.CompilerParams(vmem_limit_bytes=24 << 20),
        cost_estimate=pl.CostEstimate(
            flops=24 * 256 * 256, bytes_accessed=2 << 20, transcendentals=0
        ),
        name="blend",
    )(*scalars, *beside)


def apply_kernel(mix_ref, x_ref, *o_refs):
    half = MEMBER_TOTAL // SIDES
    states = x_ref[:, 0].reshape(MEMBER_TOTAL, WIDTH)
    center = jnp.sum(states, axis=0, keepdims=True) * (1.0 / MEMBER_TOTAL)
    updated = center + dot(mix_ref[0], states - center)
    for side in range(SIDES):
        part = updated[side * half : (side + 1) * half].reshape(RINGS, SHARE, WIDTH)
        if len(o_refs) == 1:
            o_refs[0][:, side] = part
        else:
            o_refs[side][:, 0] = part


def apply(mixed, region, states, arrays):
    sides = SIDES // arrays
    return pl.pallas_call(
        apply_kernel,
        grid=(TILE_POINTS // WIDTH,),
        in_specs=[
            pl.BlockSpec((1, MEMBER_TOTAL, MEMBER_TOTAL), lambda i: (region, 0, 0)),
            pl.BlockSpec((SHARES, 1, SHARE, WIDTH), lambda i: (0, region, 0, i)),
        ],
        out_specs=[pl.BlockSpec((RINGS, sides, SHARE, WIDTH), lambda i: (0, 0, 0, i))] * arrays,
        out_shape=[pltpu.HBM((RINGS, sides, SHARE, TILE_POINTS), jnp.float32)] * arrays,
        compiler_params=pltpu.CompilerParams(vmem_limit_bytes=24 << 20),
        cost_estimate=pl.CostEstimate(
            flops=6 * 2 * 256 * 256 * TILE_POINTS, bytes_accessed=5 << 20, transcendentals=0
        ),
        name="apply",
    )(mixed, pltpu.with_memory_space_constraint(states, pltpu.HBM))


def member_at(index, along_x, along_z):
    columns = SHARES // RINGS
    return (index // RINGS + along_x) % columns * RINGS + (index + along_z) % RINGS


RING_ORDER = (0, 4, 1, 5, 2, 6, 7, 3)


def listed_at(members, listed):
    place = jnp.zeros(members.shape, jnp.int32)
    for number, member in enumerate(listed):
        place = jnp.where(members == member, number, place)
    return place


def traded_by_all(pieces):
    return lax.all_to_all(pieces, "member", 0, 0, axis_index_groups=[ALL_LISTED], tiled=True)


def traded(pieces):
    groups = [[side * RINGS + along for along in LISTED] for side in range(SIDES)]
    return lax.all_to_all(pieces, "member", 0, 0, axis_index_groups=groups, tiled=True)


def across(pieces):
    return lax.ppermute(pieces, "member", [(i, member_at(i, 1, 0)) for i in range(SHARES)])


def from_ring(cells, states):
    def sent(piece, step):
        return lax.ppermute(
            piece, "member", [(i, member_at(i, 0, step)) for i in range(SHARES)]
        )

    pair = jnp.stack([cells, sent(cells, 4)])
    packed, pair = lax.optimization_barrier((pack(states, 0), pair))
    packed = pack(states, 1, packed)
    pieces = [sent(pair, step) for step in (1, 2, 7)]
    packed, pieces = lax.optimization_barrier((packed, pieces))
    return jnp.concatenate([pair] + pieces), packed


def from_around(near):
    count = lax.axis_size("region")
    got = []
    for shift in (1, 0, -1):
        for across in (0, 1):
            if shift == 0 and across == 0:
                got.append(near)
                continue
            pairs = [
                (g * SHARES + i, (g + shift) % count * SHARES + member_at(i, across, 0))
                for g in range(count)
                for i in range(SHARES)
            ]
            got.append(lax.ppermute(near, ("region", "member"), pairs))
    return got


def from_beside(cells):
    count = lax.axis_size("region")
    before = lax.ppermute(cells, "region", [(i, (i + 1) % count) for i in range(count)])
    after = lax.ppermute(cells, "region", [((i + 1) % count, i) for i in range(count)])
    return before, after


def body(
    prior_states,
    prior_in_sensor_space,
    sensor_readings,
    error_precisions,
    live_tallies,
    adjacent_areas,
    taper_lookup,
    blend_lookup,
    taper_factors,
):
    cycle = lax.axis_size("region")
    place = lax.axis_index("region").astype(jnp.int32)[None]
    index = lax.axis_index("member").astype(jnp.int32)
    along = (index % RINGS - jnp.array(RING_ORDER, jnp.int32)) % RINGS
    here = index // RINGS
    leave = listed_at(along, LISTED)
    leave = jnp.concatenate([leave, RINGS + leave])
    enter = jnp.concatenate([here * RINGS + along, (1 - here) * RINGS + along])
    enter = listed_at(enter, ALL_LISTED)
    here, there = here[None], 1 - here[None]
    near, packed = from_ring(prior_in_sensor_space, prior_states)
    cells = from_around(near)
    states = traded_by_all(packed)
    transforms = analysis(
        cycle,
        place,
        live_tallies,
        adjacent_areas,
        taper_factors,
        cells,
        sensor_readings,
        error_precisions,
        taper_lookup,
    )
    left, right = from_beside(transforms)
    scalars = (place, adjacent_areas, taper_factors, blend_lookup, enter, leave)
    mixed = blend(cycle, scalars, (left, transforms, right))
    (leaving,) = apply(mixed, 0, states, 1)
    first = traded(leaving)
    near, far = apply(mixed, 1, states, 2)
    both = jnp.concatenate([near, across(far)], axis=1)
    both, first = lax.optimization_barrier((both, first))
    second = traded(both)
    out = unpack(0, here, first)
    out = unpack(0, there, across(first[:, 1:]), out)
    return unpack(1, jnp.concatenate([here, there]), second, out)


def solution(mesh):
    placed = (
        P("region", "member", None, None),
        P("region", "member", None),
        P(),
        P(),
        P(),
        P(),
        P(),
        P("region", "member", None),
        P(),
    )
    return jax.shard_map(
        body,
        mesh=mesh,
        in_specs=placed,
        out_specs=P("region", "member", None, None),
        check_vma=False,
    )
```
